256 devices in a mesh: row: 8 (over y_lo, x), col: 32 (over z, y_hi, core).
Axes of the slice: x: 4, y: 4 (y_hi: 2, y_lo: 2; y = y_hi * 2 + y_lo), z: 8, core: 2. Of those that a mesh axis runs over, the one named last changes fastest.
Arguments:
- descriptors: bfloat16 [24576, 768], P(('row', 'col')), may hold values from -6 to 6
- coefficients: bfloat16 [24576, 256], P('col'), may hold values from -0.119628906 to 0.119628906
- targets: float32 [24576, 256], P(('row', 'col')), may hold values from -6 to 6
- whitening: float32 [2, 256, 256], replicated, may hold values from -1 to 2, as said below
Outputs:
- updated: float32 [24576, 24576], P('row', 'col')
- residual: float32 [24576, 256], P(('row', 'col'))
The draws below stay inside these ranges and needn't reach their ends.
Inputs may be any that keep to these rules, and one draw needn't show every extreme that they name: whitening holds two given 256 x 256 matrices; nothing more is assumed of them.
All inputs are finite; a program needn't handle non-finite values.
Results may differ from the reference program's by a relative error of at most 0.0029.
Values may be sent and summed in bfloat16 or wider, within the bound.
A program may use at most 128 MiB of HBM per device.

```python
import math
import jax
import jax.numpy as jnp
from jax import lax

F = 768
NRESP = 256
PANEL = 256
ROWS_DEV = 3072
ORDER = 24576
N_ROW = 8


def draw_descriptors(key, part):
    count = max(ORDER // 48, 4)
    groups = max(count // 16, 2)
    keys = jax.random.split(key, 6)
    assign = jax.random.randint(keys[0], (ORDER,), 0, count, dtype=jnp.int32)
    group_vecs = jax.random.truncated_normal(keys[1], -3.0, 3.0, (groups, F), jnp.float32)
    centres = 0.45 * jax.random.truncated_normal(keys[2], -3.0, 3.0, (count, F), jnp.float32)
    radius = jnp.exp(jax.random.uniform(keys[3], (count, 1), jnp.float32, math.log(0.6), math.log(1.6)))
    noise = jax.random.truncated_normal(keys[4], -3.0, 3.0, (ORDER, F), jnp.float32)
    spread = jax.random.uniform(keys[5], (ORDER, 1), jnp.float32, 0.3, 0.5)
    group_scale = 0.5
    members = jnp.take(centres * radius, assign, axis=0)
    members = members + group_scale * jnp.take(group_vecs, assign % groups, axis=0)
    return jnp.clip(members + noise * spread, -6.0, 6.0).astype(jnp.bfloat16)


def draw_whitening(key, part):
    noise = jax.random.truncated_normal(key, -4.0, 4.0, (2, PANEL, PANEL), jnp.float32)
    eye = jnp.eye(PANEL, dtype=jnp.float32)
    return (1.5 * noise + 3.0 * eye[None, :, :]) / PANEL


def level_of(key, shape, pieces, least, largest):
    level = 1.0
    for position, shards_of in pieces:
        heights = jax.random.uniform(jax.random.fold_in(jax.random.fold_in(key, 6), position), (shards_of,), jnp.float32, least / len(pieces), largest / len(pieces))
        level = level * jnp.repeat(jnp.exp(heights), shape[position] // shards_of).reshape((-1,) + (1,) * (len(shape) - 1 - position))
    return level


def scatter_about(stream_key, shape, scale, most, cuts=(), kind=jnp.bfloat16):
    array = scale * jax.random.normal(stream_key, shape, jnp.float32)
    if cuts:
        array = array * level_of(stream_key, shape, cuts, -0.22, 0.18)
    return jnp.clip(array, -most, most).astype(kind)


def setup_inputs(seed: int = 0) -> dict:
    seeds = jax.random.split(jax.random.key(seed), 5)
    descriptors = draw_descriptors(jax.random.fold_in(seeds[4], 71), 0)
    coefficients = scatter_about(seeds[1], (ORDER, NRESP), 0.02, 0.119628906, ((0, 32),))
    targets = scatter_about(seeds[2], (ORDER, NRESP), 1.0, 6.0, ((0, 256),), jnp.float32)
    whitening = draw_whitening(jax.random.fold_in(seeds[4], 71), 0)
    return dict(descriptors=descriptors, coefficients=coefficients, targets=targets, whitening=whitening)


RIDGE = 0.5


def kernel_block(left_points, right_points, left_first, right_first):
    inner = lax.dot_general(left_points, right_points, (((1,), (1,)), ((), ())), preferred_element_type=jnp.float32)
    left_sq = jnp.sum(jnp.square(left_points.astype(jnp.float32)), axis=1)
    right_sq = jnp.sum(jnp.square(right_points.astype(jnp.float32)), axis=1)
    distance = left_sq[:, None] + right_sq[None, :] - 2.0 * inner
    values = jnp.exp(-distance / (2.0 * F))
    left_ids = left_first + jnp.arange(left_points.shape[0], dtype=jnp.int32)
    right_ids = right_first + jnp.arange(right_points.shape[0], dtype=jnp.int32)
    return values + jnp.where(left_ids[:, None] == right_ids[None, :], RIDGE, 0.0)


def outer_rows(left_panel, right_panel):
    return lax.dot_general(left_panel, right_panel, (((1,), (1,)), ((), ())), preferred_element_type=jnp.float32)


def whiten(values, matrix):
    return jnp.dot(values, matrix, precision=lax.Precision.HIGHEST, preferred_element_type=jnp.float32).astype(jnp.bfloat16)


def reference(descriptors, coefficients, targets, whitening):
    panel_points = descriptors[: 2 * PANEL]
    panel_kernel = kernel_block(descriptors, panel_points, 0, 0)
    first_panel = whiten(panel_kernel[:, :PANEL], whitening[0])
    after_first = panel_kernel[:, PANEL:] - outer_rows(first_panel, first_panel[PANEL:2 * PANEL])
    second_panel = whiten(after_first, whitening[1])

    def one_block(index):
        start = (index * ROWS_DEV).astype(jnp.int32)
        block_points = lax.dynamic_slice_in_dim(descriptors, start, ROWS_DEV, 0)
        values = kernel_block(block_points, descriptors, start, 0)
        product = jnp.dot(values.astype(jnp.bfloat16), coefficients, preferred_element_type=jnp.float32)
        block_resid = lax.dynamic_slice_in_dim(targets, start, ROWS_DEV, 0) - product
        first_rows = lax.dynamic_slice_in_dim(first_panel, start, ROWS_DEV, 0)
        second_rows = lax.dynamic_slice_in_dim(second_panel, start, ROWS_DEV, 0)
        values = values - outer_rows(first_rows, first_panel)
        values = values - outer_rows(second_rows, second_panel)
        return values, block_resid

    updated, residual = lax.map(one_block, jnp.arange(N_ROW, dtype=jnp.int32))
    return updated.reshape(ORDER, ORDER), residual.reshape(ORDER, NRESP)
```

```python
import functools
import jax
import jax.numpy as jnp
from jax import lax
from jax.experimental import pallas as pl
from jax.experimental.pallas import tpu as pltpu
from jax.sharding import PartitionSpec as P

MESH = pl.DeviceIdType.MESH
SHARD, F = 96, 768
ROWS, COLS = 3072, 768
STOP = "m"


def place():
    r = lax.axis_index("row")
    c = lax.axis_index("col")
    return r % 4, r // 4, (c // 2) % 2, c // 4, c % 2


def device(x, l, h, z, k):
    return (l * 4 + x, z * 4 + h * 2 + k)


class Sender:
    def __init__(self, sems):
        self.sems = sems
        self.items = []

    def send(self, src, dst, recv, dev, cond=None):
        n = len(self.items)

        def make():
            return pltpu.make_async_remote_copy(
                src, dst, self.sems.at[n], recv, device_id=dev, device_id_type=MESH
            )

        self.items.append((make, cond))
        if cond is None:
            make().start()
        else:
            pl.when(cond)(lambda: make().start())

    def drain(self):
        for make, cond in self.items:
            if cond is None:
                make().wait_send()
            else:
                pl.when(cond)(lambda make=make: make().wait_send())


def gather_kernel(x_in, xr, xc, xp, ssem, za, zb, yb, yc, sa, sb, sc, xps, xms, yx, op, om, op2, om2, p1, p2, p3, loc):
    x, l, h, z, k = place()
    r = l * 4 + x
    c = z * 4 + h * 2 + k
    zplus, zminus = device(x, l, h, (z + 1) % 8, k), device(x, l, h, (z + 7) % 8, k)
    ypart, sib = device(x, l, 1 - h, z, k), device(x, l, h, z, 1 - k)
    xplus, xminus = device((x + 1) % 4, l, h, z, k), device((x + 3) % 4, l, h, z, k)
    yl = device(x, 1 - l, h, z, k)

    def arrived(ref, sem, cond=None):
        def wait():
            pltpu.make_async_copy(ref, ref, sem).wait()

        if cond is None:
            wait()
        else:
            pl.when(cond)(wait)

    t = 4 * r + 2 * h + k
    owner = t // 6
    is_owner = jnp.logical_and(r == 0, c < 6)
    self_piece = jnp.logical_and(r == 0, c == 0)
    bar = pltpu.get_barrier_semaphore()

    def hello(dev):
        pl.semaphore_signal(bar, inc=1, device_id=dev, device_id_type=MESH)

    for dev in (zplus, zminus, sib):
        hello(dev)
    for i in range(1, 16):
        rr = (r + i // 2) % 8
        hh = (h + i) % 2
        hello((rr, z * 4 + hh * 2 + k))
    pl.when(jnp.logical_not(self_piece))(lambda: hello((0, owner)))
    extra = jnp.where(c == 0, 47, jnp.where(c < 5, 48, 16))
    pl.semaphore_wait(bar, 18 + jnp.where(is_owner, extra, 0))

    out = Sender(ssem)

    def rows(start, n):
        return xr.at[pl.ds(pl.multiple_of(start, 16), n)]

    def first(p, hh, kk):
        return 384 * p + 96 * (2 * hh + kk)

    own = first(z, h, k)
    own_copy = pltpu.make_async_copy(x_in, rows(own, 96), loc.at[0])
    own_copy.start()
    out.send(x_in.at[pl.ds(0, 48)], rows(own, 48), yb.at[0], ypart)
    out.send(x_in, rows(own, 96), za.at[0], zplus)
    out.send(x_in, rows(own, 96), za.at[1], zminus)
    out.send(x_in.at[pl.ds(48, 48)], rows(own + 48, 48), yc.at[0], ypart)
    out.send(x_in, rows(own, 96), sa.at[0], sib)
    for j in range(0 if 'p' in STOP else 6):
        tt = 6 * c + j
        piece = jnp.logical_and(is_owner, tt < 32)
        for zz in range(8):
            here = jnp.logical_and(piece, jnp.logical_or(tt > 0, z != zz)) if (j == 0 and zz == 0) else piece
            out.send(
                x_in.at[pl.ds(16 * j, 16)],
                xp.at[tt // 4, (tt // 2) % 2, tt % 2],
                p1.at[0],
                (tt // 4, zz * 4 + tt % 4),
                here,
            )

    def mine():
        copy = pltpu.make_async_copy(x_in.at[pl.ds(0, 16)], xp.at[0, 0, 0], loc.at[1])
        copy.start()
        copy.wait()

    pl.when(self_piece)(mine)

    def plane(s, d):
        return (z + 16 - d * s) % 8

    arrived(rows(first(z, 1 - h, k), 48), yb.at[0])
    part = rows(first(z, 1 - h, k), 48)
    out.send(part, part, zb.at[0], zplus)
    out.send(part, part, zb.at[1], zminus)
    out.send(part, part, sb.at[0], sib)

    def late(s):
        for n, d in enumerate((1, -1)):
            if s in (0, 4) and n == 1:
                continue
            i = 0 if s == 0 else (2 * s - 1 + n)
            p = plane(s, d)
            piece = rows(first(p, 1 - h, k) + 48, 48)
            arrived(piece, yc.at[i])
            out.send(piece, piece, sc.at[i], sib)
        for n, d in enumerate((1, -1)):
            if s in (0, 4) and n == 1:
                continue
            i = 0 if s == 0 else (2 * s - 1 + n)
            p = plane(s, d)
            arrived(rows(first(p, h, 1 - k), 96), sa.at[i])
            arrived(rows(first(p, 1 - h, 1 - k), 48), sb.at[i])
            arrived(rows(first(p, 1 - h, 1 - k) + 48, 48), sc.at[i])

    for s in range(1, 5):
        if s < 4:
            for n, d in enumerate((1, -1)):
                i = 2 * s - 1 + n
                p = plane(s, d)
                a = rows(first(p, h, k), 96)
                arrived(a, za.at[i - 1])
                if s < 3:
                    out.send(a, a, za.at[i + 1], zplus if d == 1 else zminus)
                c_half = rows(first(p, h, k) + 48, 48)
                out.send(c_half, c_half, yc.at[i], ypart)
                out.send(a, a, sa.at[i], sib)
            if s == 3:
                da = 1 - 2 * k
                a = rows(first((z + 16 - 3 * da) % 8, h, k), 96)
                out.send(a, a, za.at[6], device(x, l, h, (z + 8 + da) % 8, k))
            for n, d in enumerate((1, -1)):
                i = 2 * s - 1 + n
                p = plane(s, d)
                b = rows(first(p, 1 - h, k), 48)
                arrived(b, zb.at[i - 1])
                if s < 3:
                    out.send(b, b, zb.at[i + 1], zplus if d == 1 else zminus)
                out.send(b, b, sb.at[i], sib)
            if s == 3:
                b = rows(first((z + 16 + 3 * da) % 8, 1 - h, k), 48)
                out.send(b, b, zb.at[6], device(x, l, h, (z + 8 - da) % 8, k))
        else:
            p = plane(4, 1)
            a = rows(first(p, h, k), 96)
            arrived(a, za.at[6])
            c_half = rows(first(p, h, k) + 48, 48)
            out.send(c_half, c_half, yc.at[7], ypart)
            out.send(a, a, sa.at[7], sib)
            b = rows(first(p, 1 - h, k), 48)
            arrived(b, zb.at[6])
            out.send(b, b, sb.at[7], sib)
        if 'l' in STOP:
            pass
        elif 'm' in STOP:
            if s >= 2: late(s - 2)
        else:
            late(s - 1)
        if s == 1 and 'p' not in STOP:
            piece = xp.at[r, h, k]
            arrived(piece, p1.at[0], jnp.logical_not(self_piece))
            for i in range(1, 16):
                rr = (r + i // 2) % 8
                hh = (h + i) % 2
                out.send(piece, piece, p2.at[i - 1], (rr, z * 4 + hh * 2 + k))
        if s == 3 and 'p' not in STOP:
            for i in range(1, 16):
                rr = (r + 8 - i // 2) % 8
                hh = (h + i) % 2
                arrived(xp.at[rr, hh, k], p2.at[i - 1])
            mine_all = xp.at[:, :, k]
            out.send(mine_all, mine_all, p3.at[0], sib)
    own_copy.wait()
    for q in (range(5) if 'l' in STOP else (3, 4) if 'm' in STOP else (4,)): late(q)

    if 'c' in STOP:
        out.drain()
        return
    xs, ls = z % 4, z // 4
    q = (x + 4 - xs) % 4
    line = l == ls
    source = jnp.logical_and(line, q == 0)
    for_me = rows(768 * (2 * h + k), 768)
    keep = pltpu.make_async_copy(for_me, xc, loc.at[2])
    pl.when(source)(lambda: keep.start())
    pl.when(source)(lambda: keep.wait())

    def block(start, n):
        return xc.at[pl.ds(pl.multiple_of(start, 16), n)]

    def inside(i):
        return jnp.logical_and(line, jnp.logical_and(i >= 0, i < 8))

    qm = (4 - q) % 4
    for tau in range(11):
        i = tau - q
        u = (i + 4) % 4
        ok = inside(i)
        ic = jnp.clip(i, 0, 7)
        j = ic // 4
        piece = block(384 * j + 48 * u, 48)
        arrived(piece, xps.at[ic], jnp.logical_and(ok, q != 0))
        out.send(piece, piece, xps.at[ic], xplus, jnp.logical_and(ok, q != 3))
        out.send(piece, piece, yx.at[2 * j + u % 2], yl, jnp.logical_and(ok, q == jnp.where(u < 2, 1, 2)))
        i = tau - qm
        u = (i + 4) % 4
        ok = inside(i)
        ic = jnp.clip(i, 0, 7)
        j = ic // 4
        piece = block(384 * j + 192 + 48 * u, 48)
        arrived(piece, xms.at[ic], jnp.logical_and(ok, q != 0))
        out.send(piece, piece, xms.at[ic], xminus, jnp.logical_and(ok, q != 1))
        out.send(piece, piece, yx.at[2 * j + u % 2], yl, jnp.logical_and(ok, q == jnp.where(u < 2, 3, 0)))
    other = jnp.logical_not(line)
    b0 = (q + 3) % 4
    bm, bp = (q + 2) % 4, q
    for i in range(4):
        piece = block(384 * (i // 2) + 96 * b0 + 48 * (i % 2), 48)
        arrived(piece, yx.at[i], other)
        out.send(piece, piece, op.at[i], xplus, other)
        out.send(piece, piece, om.at[i], xminus, other)
    for j in range(2):
        for u in range(2):
            piece = block(384 * j + 96 * bm + 48 * u, 48)
            arrived(piece, op.at[2 * j + u], other)
            if u == 0:
                out.send(piece, piece, op2.at[j], xplus, other)
            piece = block(384 * j + 96 * bp + 48 * u, 48)
            arrived(piece, om.at[2 * j + u], other)
            if u == 1:
                out.send(piece, piece, om2.at[j], xminus, other)
    bo = (q + 1) % 4
    for j in range(2):
        arrived(block(384 * j + 96 * bo, 48), op2.at[j], other)
        arrived(block(384 * j + 96 * bo + 48, 48), om2.at[j], other)
    if 'p' not in STOP: arrived(xp.at[:, :, 1 - k], p3.at[0])
    out.drain()


def gather(descriptors):
    dma = pltpu.SemaphoreType.DMA
    vm = pl.BlockSpec(memory_space=pltpu.VMEM)
    return pl.pallas_call(
        gather_kernel,
        out_shape=(
            jax.ShapeDtypeStruct((ROWS, F), jnp.bfloat16),
            jax.ShapeDtypeStruct((COLS, F), jnp.bfloat16),
            jax.ShapeDtypeStruct((8, 2, 2, 16, F), jnp.bfloat16),
        ),
        in_specs=[vm],
        out_specs=(vm, vm, vm),
        scratch_shapes=[dma((240,)), dma((7,)), dma((7,)), dma((1,)), dma((8,)), dma((8,)), dma((8,)), dma((8,)),
                        dma((8,)), dma((8,)), dma((4,)), dma((4,)), dma((4,)), dma((2,)), dma((2,)),
                        dma((1,)), dma((15,)), dma((1,)), dma((3,))],
        compiler_params=pltpu.CompilerParams(collective_id=0, has_side_effects=True, vmem_limit_bytes=40 << 20),
        name="gather",
    )(descriptors)


RIDGE = 0.5
NRESP = 256
PANEL = 256
BLK = 384
BF, F32 = jnp.bfloat16, jnp.float32


def dot_t(a, b):
    return lax.dot_general(a, b, (((1,), (1,)), ((), ())), preferred_element_type=F32)


def dot(a, b):
    return jnp.dot(a, b, preferred_element_type=F32)


def halves(a):
    high = a.astype(BF)
    return high, (a - high.astype(F32)).astype(BF)


def whiten(values, w_high, w_low):
    high, low = halves(values)
    return (dot(high, w_high) + dot(high, w_low) + dot(low, w_high)).astype(BF)


def square_sums(points):
    wide = points.astype(F32)
    return jnp.sum(wide * wide, axis=1, keepdims=True)


def as_row(column):
    n = column.shape[0]
    return jnp.transpose(jnp.broadcast_to(column, (n, 128)))[0:1, :]


def gaussian(left, right, left_sums, right_sums):
    distance = left_sums + right_sums - 2.0 * dot_t(left, right)
    return jnp.exp(distance * (-1.0 / (2.0 * F)))


def with_ridge(values, gap):
    i = lax.broadcasted_iota(jnp.int32, values.shape, 0)
    j = lax.broadcasted_iota(jnp.int32, values.shape, 1)
    return values + jnp.where(i - j == gap, RIDGE, 0.0)


def tile_kernel(xr, xc, xp, coef, w, upd, part, top, pc, sp, sj, wh, wl):
    b = pl.program_id(0)
    row0 = lax.axis_index("row") * ROWS + b * BLK
    col0 = lax.axis_index("col") * COLS

    def panels(points, sums, first):
        k0 = with_ridge(gaussian(points, xp[...], sums, sp[...]), -first)
        p1 = whiten(k0[:, :PANEL], wh[0], wl[0])
        k1 = k0[:, PANEL:] - dot_t(p1, top[...])
        return p1, whiten(k1, wh[1], wl[1])

    @pl.when(b == 0)
    def _():
        for i in range(2):
            high, low = halves(w[i])
            wh[i] = high
            wl[i] = low
        sp[...] = as_row(square_sums(xp[...]))
        sj[...] = as_row(square_sums(xc[...]))
        lower = xp[PANEL:, :]
        k0 = gaussian(lower, xp[:PANEL, :], square_sums(lower), sp[:, :PANEL])
        top[...] = whiten(k0, wh[0], wl[0])
        for i in range(2):
            points = xc[pl.ds(BLK * i, BLK), :]
            p1, p2 = panels(points, square_sums(points), col0 + BLK * i)
            pc[pl.ds(BLK * i, BLK), :PANEL] = p1
            pc[pl.ds(BLK * i, BLK), PANEL:] = p2

    points = xr[...]
    sums = square_sums(points)
    kern = with_ridge(gaussian(points, xc[...], sums, sj[...]), col0 - row0)
    part[...] = dot(kern.astype(BF), coef[...])
    p1, p2 = panels(points, sums, row0)
    upd[...] = kern - dot_t(p1, pc[:, :PANEL]) - dot_t(p2, pc[:, PANEL:])


def tile(xr, xc, xp, coef, w):
    whole = lambda *shape: pl.BlockSpec(shape, lambda b: (0,) * len(shape))
    return pl.pallas_call(
        tile_kernel,
        grid=(ROWS // BLK,),
        out_shape=(jax.ShapeDtypeStruct((ROWS, COLS), F32), jax.ShapeDtypeStruct((ROWS, NRESP), F32)),
        in_specs=[pl.BlockSpec((BLK, F), lambda b: (b, 0)), whole(COLS, F), whole(2 * PANEL, F), whole(COLS, NRESP), whole(2, PANEL, PANEL)],
        out_specs=(pl.BlockSpec((BLK, COLS), lambda b: (b, 0)), pl.BlockSpec((BLK, NRESP), lambda b: (b, 0))),
        scratch_shapes=[pltpu.VMEM((PANEL, PANEL), BF), pltpu.VMEM((COLS, 2 * PANEL), BF), pltpu.VMEM((1, 2 * PANEL), F32),
                        pltpu.VMEM((1, COLS), F32), pltpu.VMEM((2, PANEL, PANEL), BF), pltpu.VMEM((2, PANEL, PANEL), BF)],
        compiler_params=pltpu.CompilerParams(dimension_semantics=("arbitrary",), vmem_limit_bytes=50 << 20),
        name="tile",
    )(xr, xc, xp, coef, w)


def reduce_kernel(part, targets, res, sbuf, rbuf, pbuf, ssem, s1, s2):
    x, l, h, z, k = place()
    sib = device(x, l, h, z, 1 - k)
    peers = [((z + i // 2) % 8, (h + i) % 2) for i in range(16)]
    bar = pltpu.get_barrier_semaphore()
    for i in range(1, 16):
        zz, hh = peers[i]
        pl.semaphore_signal(bar, inc=1, device_id=device(x, l, hh, zz, k), device_id_type=MESH)
    pl.semaphore_signal(bar, inc=1, device_id=sib, device_id_type=MESH)
    pl.semaphore_wait(bar, 16)
    out = Sender(ssem)
    order = [4, 5, 3, 6, 2, 7, 1, 0]
    for d in order:
        zz = (z + d) % 8
        out.send(part.at[zz, :, 1 - k], pbuf.at[zz], s1.at[d], sib)
    for d in order:
        zz = (z + d) % 8
        pltpu.make_async_copy(pbuf.at[zz], pbuf.at[zz], s1.at[d]).wait()
        for i in (2 * d, 2 * d + 1):
            hh = (h + i) % 2
            total = part[zz, hh, k] + pbuf[zz, hh]
            sbuf[i] = total.astype(BF)
            if i > 0:
                out.send(sbuf.at[i], rbuf.at[i], s2.at[i], device(x, l, hh, zz, k))
    acc = targets[...] - sbuf[0].astype(F32)
    for i in range(1, 16):
        pltpu.make_async_copy(rbuf.at[i], rbuf.at[i], s2.at[i]).wait()
        acc = acc - rbuf[i].astype(F32)
    res[...] = acc
    out.drain()


def reduce(part, targets):
    dma = pltpu.SemaphoreType.DMA
    vm = pl.BlockSpec(memory_space=pltpu.VMEM)
    return pl.pallas_call(
        reduce_kernel,
        out_shape=jax.ShapeDtypeStruct((SHARD, NRESP), F32),
        in_specs=[vm, vm],
        out_specs=vm,
        scratch_shapes=[pltpu.VMEM((16, SHARD, NRESP), BF), pltpu.VMEM((16, SHARD, NRESP), BF), pltpu.VMEM((8, 2, SHARD, NRESP), F32),
                        dma((40,)), dma((8,)), dma((16,))],
        compiler_params=pltpu.CompilerParams(collective_id=1, has_side_effects=True, vmem_limit_bytes=40 << 20),
        name="reduce",
    )(part.reshape(8, 2, 2, SHARD, NRESP), targets)


def body(descriptors, coefficients, targets, whitening):
    xr, xc, xp = gather(descriptors)
    updated, part = tile(xr, xc, xp.reshape(2 * PANEL, F), coefficients, whitening)
    return updated, reduce(part, targets)


def solution(mesh):
    in_specs = (P(("row", "col"), None), P("col", None), P(("row", "col"), None), P())
    out_specs = (P("row", "col"), P(("row", "col"), None))
    return jax.shard_map(body, mesh=mesh, in_specs=in_specs, out_specs=out_specs, check_vma=False)
```

```python
import jax
import jax.numpy as jnp
from jax import lax
from jax.experimental import pallas as pl
from jax.experimental.pallas import tpu as pltpu
from jax.sharding import PartitionSpec as P

MESH = pl.DeviceIdType.MESH
SHARD, F = 96, 768
ROWS, COLS = 3072, 768
RIDGE = 0.5
NRESP = 256
PANEL = 256
BLK = 384
HALF = 48
BF, F32 = jnp.bfloat16, jnp.float32


def place():
    r = lax.axis_index("row")
    c = lax.axis_index("col")
    return r % 4, r // 4, (c // 2) % 2, c // 4, c % 2


def device(x, l, h, z, k):
    return (l * 4 + x, z * 4 + h * 2 + k)


def both(*conds):
    out = conds[0]
    for cond in conds[1:]:
        out = jnp.logical_and(out, cond)
    return out


def dot_t(a, b):
    return lax.dot_general(a, b, (((1,), (1,)), ((), ())), preferred_element_type=F32)


def dot(a, b):
    return jnp.dot(a, b, preferred_element_type=F32)


def halves(a):
    high = a.astype(BF)
    return high, (a - high.astype(F32)).astype(BF)


def whiten(values, w_high, w_low):
    high, low = halves(values)
    return (dot(high, w_high) + dot(high, w_low) + dot(low, w_high)).astype(BF)


def square_sums(points):
    wide = points.astype(F32)
    return jnp.sum(wide * wide, axis=1, keepdims=True)


def as_row(column):
    n = column.shape[0]
    return jnp.transpose(jnp.broadcast_to(column, (n, 128)))[0:1, :]


def gaussian(left, right, left_sums, right_sums):
    distance = left_sums + right_sums - 2.0 * dot_t(left, right)
    return jnp.exp(distance * (-1.0 / (2.0 * F)))


def with_ridge(values, gap):
    i = lax.broadcasted_iota(jnp.int32, values.shape, 0)
    j = lax.broadcasted_iota(jnp.int32, values.shape, 1)
    return values + jnp.where(i - j == gap, RIDGE, 0.0)


class Sender:
    def __init__(self, sems):
        self.sems = sems
        self.items = []

    def send(self, src, dst, recv, dev, cond=None):
        n = len(self.items)

        def make():
            return pltpu.make_async_remote_copy(
                src, dst, self.sems.at[n], recv, device_id=dev, device_id_type=MESH
            )

        self.items.append((make, cond))
        if cond is None:
            make().start()
        else:
            pl.when(cond)(lambda: make().start())

    def drain(self):
        for make, cond in self.items:
            if cond is None:
                make().wait_send()
            else:
                pl.when(cond)(lambda make=make: make().wait_send())


def arrived(ref, sem, cond=None):
    def wait():
        pltpu.make_async_copy(ref, ref, sem).wait()

    if cond is None:
        wait()
    else:
        pl.when(cond)(wait)


def main_kernel(
    x_in, coef_in, w_in, t_in,
    kern, pr, pc, res,
    xr, xc, xp, coef, w, t, top, sp, sj, wh, wl, part, pbuf, sbuf, rbuf,
    ssem, za, yb, yc, sa, sb, sc, xps, xms, yx, op, om, op2, om2, xsend, p1, p2, p3, loc, s1, s1s, s2, s2s,
):
    x, l, h, z, k = place()
    r = l * 4 + x
    c = z * 4 + h * 2 + k
    zplus, zminus = device(x, l, h, (z + 1) % 8, k), device(x, l, h, (z + 7) % 8, k)
    ypart, sib = device(x, l, 1 - h, z, k), device(x, l, h, z, 1 - k)
    xplus, xminus = device((x + 1) % 4, l, h, z, k), device((x + 3) % 4, l, h, z, k)
    yl = device(x, 1 - l, h, z, k)
    t_of_me = 4 * r + 2 * h + k
    is_owner = both(r == 0, c < 6)
    self_piece = both(r == 0, c == 0)
    not_self = jnp.logical_not(self_piece)

    def first(p, hh, kk):
        return 384 * p + 96 * (2 * hh + kk)

    def rows(start, n):
        return xr.at[pl.ds(pl.multiple_of(start, 16), n)]

    own = first(z, h, k)
    fetches = [
        pltpu.make_async_copy(x_in, rows(own, 96), loc.at[0]),
        pltpu.make_async_copy(coef_in, coef, loc.at[1]),
        pltpu.make_async_copy(w_in, w, loc.at[2]),
        pltpu.make_async_copy(t_in, t, loc.at[3]),
    ]
    for fetch in fetches:
        fetch.start()

    bar = pltpu.get_barrier_semaphore()

    def hello(dev):
        pl.semaphore_signal(bar, inc=1, device_id=dev, device_id_type=MESH)

    for i in range(1, 16):
        hello(((r + i // 2) % 8, z * 4 + ((h + i) % 2) * 2 + k))
    for i in range(2, 16):
        hello(device(x, l, (h + i) % 2, (z + i // 2) % 8, k))
    hello(sib)
    pl.when(not_self)(lambda: hello((0, t_of_me // 6)))
    extra = jnp.where(c == 0, 47, jnp.where(c < 5, 48, 16))
    pl.semaphore_wait(bar, 30 + jnp.where(is_owner, extra, 0))

    out = Sender(ssem)

    def piece(p, n):
        return rows(first(p, h, k) + HALF * n if n < 2 else first(p, 1 - h, k), HALF)

    def plane(s, d):
        return (z + 16 - d * s) % 8

    def slot(s, n):
        return 0 if s == 0 else 2 * s - 1 + n

    first_copy = fetches[0]
    mine = [x_in.at[pl.ds(HALF * n, HALF)] for n in range(2)]
    out.send(mine[0], piece(z, 0), yb.at[0], ypart)
    for n in range(2):
        out.send(mine[n], piece(z, n), za.at[n], zplus)
        out.send(mine[n], piece(z, n), za.at[3 + n], zminus)
    out.send(mine[1], piece(z, 1), yc.at[0], ypart)
    out.send(x_in, rows(own, 96), sa.at[0], sib)
    arrived(piece(z, 2), yb.at[0])
    out.send(piece(z, 2), piece(z, 2), za.at[2], zplus)
    out.send(piece(z, 2), piece(z, 2), za.at[5], zminus)
    out.send(piece(z, 2), piece(z, 2), sb.at[0], sib)

    def late(s):
        pairs = [(n, d) for n, d in enumerate((1, -1)) if not (s in (0, 4) and n == 1)]
        for n, d in pairs:
            i, p = slot(s, n), plane(s, d)
            got = rows(first(p, 1 - h, k) + HALF, HALF)
            arrived(got, yc.at[i])
            out.send(got, got, sc.at[i], sib)
        for n, d in pairs:
            i, p = slot(s, n), plane(s, d)
            arrived(rows(first(p, h, 1 - k), 96), sa.at[i])
            arrived(rows(first(p, 1 - h, 1 - k), HALF), sb.at[i])
            arrived(rows(first(p, 1 - h, 1 - k) + HALF, HALF), sc.at[i])

    xs, ls = z % 4, z // 4
    q = (x + 4 - xs) % 4
    line = l == ls
    other = jnp.logical_not(line)
    hops_plus, hops_minus = q, (4 - q) % 4
    near = jnp.minimum(q, 4 - q)
    b0, bm, bp, bo = (q + 3) % 4, (q + 2) % 4, q, (q + 1) % 4

    def gap(j):
        away = (4 * h + 2 * k + j + 8 - z) % 8
        return jnp.minimum(away, 8 - away)

    def block(j, b, half=None):
        start = 384 * j + 96 * b + (0 if half is None else HALF * half)
        return xc.at[pl.ds(pl.multiple_of(start, 16), 96 if half is None else HALF)]

    def raw(j, b):
        return rows(384 * (4 * h + 2 * k + j) + 96 * b, 96)

    def remote(src, dst, n, recv, dev):
        return pltpu.make_async_remote_copy(src, dst, xsend.at[n], recv, device_id=dev, device_id_type=MESH)

    def column_stage(s):
        def step(j, carry):
            g = gap(j)

            @pl.when(both(line, g + hops_plus == s))
            def _():
                for u in range(2):
                    got = block(j, u)
                    arrived(got, xps.at[2 * j + u], q != 0)

                    @pl.when(q == 0)
                    def _():
                        remote(raw(j, u), got, 5 * j + u, xps.at[2 * j + u], xplus).start()

                    @pl.when(both(q != 0, q != 3))
                    def _():
                        remote(got, got, 5 * j + u, xps.at[2 * j + u], xplus).start()

                    @pl.when(q == u + 1)
                    def _():
                        remote(got, got, 5 * j + 4, yx.at[j], yl).start()

            @pl.when(both(line, g + hops_minus == s))
            def _():
                for u in range(2):
                    got = block(j, 2 + u)
                    arrived(got, xms.at[2 * j + u], q != 0)

                    @pl.when(q == 0)
                    def _():
                        remote(raw(j, 2 + u), got, 5 * j + 2 + u, xms.at[2 * j + u], xminus).start()

                    @pl.when(both(q != 0, q != 1))
                    def _():
                        remote(got, got, 5 * j + 2 + u, xms.at[2 * j + u], xminus).start()

                    if u == 0:
                        @pl.when(q == 3)
                        def _():
                            remote(got, got, 5 * j + 4, yx.at[j], yl).start()
                    else:
                        @pl.when(q == 0)
                        def _():
                            remote(raw(j, 3), got, 5 * j + 4, yx.at[j], yl).start()

            @pl.when(both(other, g + near + 1 == s))
            def _():
                got = block(j, b0)
                arrived(got, yx.at[j])
                remote(got, got, 5 * j, op.at[j], xplus).start()
                remote(got, got, 5 * j + 1, om.at[j], xminus).start()

            @pl.when(both(other, g + jnp.where(q % 2 == 0, 3, 4) == s))
            def _():
                arrived(block(j, bm), op.at[j])
                remote(block(j, bm, 0), block(j, bm, 0), 5 * j + 2, op2.at[j], xplus).start()
                arrived(block(j, bp), om.at[j])
                remote(block(j, bp, 1), block(j, bp, 1), 5 * j + 3, om2.at[j], xminus).start()

            return carry

        lax.fori_loop(0, 2, step, 0)

    def columns_end():
        def step(j, carry):
            @pl.when(other)
            def _():
                arrived(block(j, bo, 0), op2.at[j])
                arrived(block(j, bo, 1), om2.at[j])
                remote(block(j, 0), block(j, 0), 5 * j, op.at[j], xplus).wait_send()
                remote(block(j, 0), block(j, 0), 5 * j + 1, om.at[j], xminus).wait_send()
                remote(block(j, 0, 0), block(j, 0, 0), 5 * j + 2, op2.at[j], xplus).wait_send()
                remote(block(j, 0, 0), block(j, 0, 0), 5 * j + 3, om2.at[j], xminus).wait_send()

            for u in range(2):
                @pl.when(both(line, q != 3))
                def _():
                    remote(block(j, u), block(j, u), 5 * j + u, xps.at[0], xplus).wait_send()

                @pl.when(both(line, q != 1))
                def _():
                    remote(block(j, u), block(j, u), 5 * j + 2 + u, xms.at[0], xminus).wait_send()

            @pl.when(line)
            def _():
                remote(block(j, 0), block(j, 0), 5 * j + 4, yx.at[0], yl).wait_send()

            return carry

        lax.fori_loop(0, 2, step, 0)

    def panel_points_out():
        for j in range(6):
            tt = 6 * c + j
            has = both(is_owner, tt < 32)
            for zz in range(8):
                out.send(
                    x_in.at[pl.ds(16 * j, 16)],
                    xp.at[tt // 4, (tt // 2) % 2, tt % 2],
                    p1.at[0],
                    (tt // 4, zz * 4 + tt % 4),
                    both(has, jnp.logical_or(tt > 0, z != zz)) if (j == 0 and zz == 0) else has,
                )

        @pl.when(self_piece)
        def _():
            keep = pltpu.make_async_copy(x_in.at[pl.ds(0, 16)], xp.at[0, 0, 0], loc.at[4])
            keep.start()
            keep.wait()

    def panel_points_plane():
        got = xp.at[r, h, k]
        arrived(got, p1.at[0], not_self)
        for i in range(1, 16):
            out.send(got, got, p2.at[i - 1], ((r + i // 2) % 8, z * 4 + ((h + i) % 2) * 2 + k))

    def panel_points_chip():
        for i in range(1, 16):
            arrived(xp.at[(r + 8 - i // 2) % 8, (h + i) % 2, k], p2.at[i - 1])
        got = xp.at[:, :, k]
        out.send(got, got, p3.at[0], sib)

    for s in range(1, 5):
        if s < 4:
            for n in range(3):
                for e, d in enumerate((1, -1)):
                    got = piece(plane(s, d), n)
                    i = slot(s, e)
                    arrived(got, za.at[6 * (s - 1) + 3 * e + n])
                    if s < 3:
                        out.send(got, got, za.at[6 * s + 3 * e + n], zplus if d == 1 else zminus)
                    if n == 1:
                        out.send(got, got, yc.at[i], ypart)
                        whole = rows(first(plane(s, d), h, k), 96)
                        out.send(whole, whole, sa.at[i], sib)
                    if n == 2:
                        out.send(got, got, sb.at[i], sib)
                if s == 3:
                    d = (1 - 2 * k) if n < 2 else (2 * k - 1)
                    got = piece((z + 16 - 3 * d) % 8, n)
                    out.send(got, got, za.at[18 + n], device(x, l, h, (z + 8 + d) % 8, k))
        else:
            for n in range(3):
                got = piece(plane(4, 1), n)
                arrived(got, za.at[18 + n])
                if n == 1:
                    out.send(got, got, yc.at[7], ypart)
                    whole = rows(first(plane(4, 1), h, k), 96)
                    out.send(whole, whole, sa.at[7], sib)
                if n == 2:
                    out.send(got, got, sb.at[7], sib)
        if s == 1:
            panel_points_out()
            first_copy.wait()
        late(s - 1)
        column_stage(s - 1)
        if s == 3:
            panel_points_plane()
    late(4)
    keep = pltpu.make_async_copy(rows(768 * (2 * h + k), 768), xc, loc.at[4])
    source = both(line, q == 0)
    column_stage(4)
    pl.when(source)(lambda: keep.start())
    for fetch in fetches[1:]:
        fetch.wait()
    for i in range(2):
        high, low = halves(w[i])
        wh[i] = high
        wl[i] = low
    for s in range(5, 9):
        column_stage(s)
    pl.when(source)(lambda: keep.wait())
    columns_end()
    panel_points_chip()

    sj[...] = as_row(square_sums(xc[...]))
    row_first = r * ROWS
    col_first = c * COLS

    def turn(i):
        return (4 + ((i + 1) // 2) * (2 * (i % 2) - 1)) % 8

    def to_sib(i):
        zz = (z + turn(i)) % 8
        return pltpu.make_async_remote_copy(
            part.at[zz, :, 1 - k], pbuf.at[zz], s1s.at[i], s1.at[i], device_id=sib, device_id_type=MESH
        )

    def to_owner(i, g):
        d = turn(i)
        zz = (z + d) % 8
        n = 2 * d + g
        return pltpu.make_async_remote_copy(
            sbuf.at[n], rbuf.at[n], s2s.at[n], s2.at[n], device_id=device(x, l, (h + g) % 2, zz, k), device_id_type=MESH
        )

    def exchange(i):
        @pl.when(both(i >= 1, i < 9))
        def _():
            to_sib(i - 1).start()

        @pl.when(both(i >= 3, i < 11))
        def _():
            for g in range(2):
                pl.when(jnp.logical_or(i != 10, g != 0))(lambda g=g: to_owner(i - 3, g).start())

    def chip_sum(i):
        @pl.when(both(i >= 2, i < 10))
        def _():
            d = turn(i - 2)
            zz = (z + d) % 8
            arrived(pbuf.at[zz], s1.at[i - 2])
            for g in range(2):
                hh = (h + g) % 2
                sbuf[2 * d + g] = (part[zz, hh, k] + pbuf[zz, hh]).astype(BF)

    def tile_step(i, carry):
        exchange(i)
        b = (z + turn(i)) % 8
        span = pl.ds(pl.multiple_of(b * BLK, BLK), BLK)
        points = xr[span, :]
        values = with_ridge(gaussian(points, xc[...], square_sums(points), sj[...]), col_first - row_first - b * BLK)
        kern[span, :] = values
        part[b] = dot(values.astype(BF), coef[...]).reshape(2, 2, SHARD, NRESP)
        chip_sum(i)
        return carry

    lax.fori_loop(0, 8, tile_step, 0)

    arrived(xp.at[:, :, 1 - k], p3.at[0])
    heads = xp.reshape(2 * PANEL, F)
    sp[...] = as_row(square_sums(heads[...]))
    lower = heads[PANEL:, :]
    top[...] = whiten(gaussian(lower, heads[:PANEL, :], square_sums(lower), sp[:, :PANEL]), wh[0], wl[0])

    def panels(points, start):
        k0 = with_ridge(gaussian(points, heads[...], square_sums(points), sp[...]), -start)
        p1 = whiten(k0[:, :PANEL], wh[0], wl[0])
        return p1, whiten(k0[:, PANEL:] - dot_t(p1, top[...]), wh[1], wl[1])

    def panel_step(b, carry):
        exchange(b + 8)
        span = pl.ds(pl.multiple_of(b * BLK, BLK), BLK)
        p1, p2 = panels(xr[span, :], row_first + b * BLK)
        pr[span, :PANEL] = p1
        pr[span, PANEL:] = p2
        chip_sum(b + 8)
        return carry

    lax.fori_loop(0, 8, panel_step, 0)

    def panel_cols(j, carry):
        span = pl.ds(pl.multiple_of(j * BLK, BLK), BLK)
        p1, p2 = panels(xc[span, :], col_first + j * BLK)
        pc[span, :PANEL] = p1
        pc[span, PANEL:] = p2
        return carry

    lax.fori_loop(0, 2, panel_cols, 0)

    acc = t[...] - sbuf[0].astype(F32)
    for n in range(2, 16):
        arrived(rbuf.at[n], s2.at[n])
        acc = acc - rbuf[n].astype(F32)
    arrived(rbuf.at[1], s2.at[1])
    res[...] = acc - rbuf[1].astype(F32)
    for i in range(8):
        to_sib(i).wait_send()
        for g in range(2):
            if i != 7 or g != 0:
                to_owner(i, g).wait_send()
    out.drain()


def update_kernel(kern, pr, pc, upd, buf, sem):
    def copy(b, n):
        return pltpu.make_async_copy(buf.at[n], upd.at[pl.ds(pl.multiple_of(b * BLK, BLK), BLK)], sem.at[n])

    def step(b, carry):
        n = b % 2
        pl.when(b >= 2)(lambda: copy(b - 2, n).wait())
        span = pl.ds(pl.multiple_of(b * BLK, BLK), BLK)
        buf[n] = kern[span, :] - dot_t(pr[span, :PANEL], pc[:, :PANEL]) - dot_t(pr[span, PANEL:], pc[:, PANEL:])
        copy(b, n).start()
        return carry

    lax.fori_loop(0, 8, step, 0)
    copy(6, 0).wait()
    copy(7, 1).wait()


def body(descriptors, coefficients, targets, whitening):
    dma = pltpu.SemaphoreType.DMA
    vm = pl.BlockSpec(memory_space=pltpu.VMEM)
    hbm = pl.BlockSpec(memory_space=pltpu.HBM)
    V = pltpu.VMEM
    kern, pr, pc, residual = pl.pallas_call(
        main_kernel,
        out_shape=(
            jax.ShapeDtypeStruct((ROWS, COLS), F32),
            jax.ShapeDtypeStruct((ROWS, 2 * PANEL), BF),
            jax.ShapeDtypeStruct((COLS, 2 * PANEL), BF),
            jax.ShapeDtypeStruct((SHARD, NRESP), F32),
        ),
        in_specs=[hbm] * 4,
        out_specs=(vm, vm, vm, vm),
        scratch_shapes=[
            V((ROWS, F), BF), V((COLS, F), BF), V((8, 2, 2, 16, F), BF), V((COLS, NRESP), BF), V((2, PANEL, PANEL), F32),
            V((SHARD, NRESP), F32), V((PANEL, PANEL), BF), V((1, 2 * PANEL), F32), V((1, COLS), F32),
            V((2, PANEL, PANEL), BF), V((2, PANEL, PANEL), BF), V((8, 2, 2, SHARD, NRESP), F32),
            V((8, 2, SHARD, NRESP), F32), V((16, SHARD, NRESP), BF), V((16, SHARD, NRESP), BF),
            dma((180,)), dma((21,)), dma((1,)), dma((8,)), dma((8,)), dma((8,)), dma((8,)), dma((4,)), dma((4,)), dma((2,)),
            dma((2,)), dma((2,)), dma((2,)), dma((2,)), dma((10,)), dma((1,)), dma((15,)), dma((1,)), dma((5,)),
            dma((8,)), dma((8,)), dma((16,)), dma((16,)),
        ],
        compiler_params=pltpu.CompilerParams(collective_id=0, has_side_effects=True, vmem_limit_bytes=26 << 20),
        name="main",
    )(descriptors, coefficients, whitening, targets)
    updated = pl.pallas_call(
        update_kernel,
        out_shape=jax.ShapeDtypeStruct((ROWS, COLS), F32),
        in_specs=[vm] * 3,
        out_specs=hbm,
        scratch_shapes=[V((2, BLK, COLS), F32), dma((2,))],
        compiler_params=pltpu.CompilerParams(vmem_limit_bytes=16 << 20),
        name="update",
    )(kern, pr, pc)
    return updated, residual


def solution(mesh):
    in_specs = (P(("row", "col"), None), P("col", None), P(("row", "col"), None), P())
    out_specs = (P("row", "col"), P(("row", "col"), None))
    return jax.shard_map(body, mesh=mesh, in_specs=in_specs, out_specs=out_specs, check_vma=False)
```

```python
import jax
import jax.numpy as jnp
from jax import lax
from jax.experimental import pallas as pl
from jax.experimental.pallas import tpu as pltpu
from jax.sharding import PartitionSpec as P

MESH = pl.DeviceIdType.MESH
SHARD, F = 96, 768
ROWS, COLS = 3072, 768
RIDGE = 0.5
NRESP = 256
PANEL = 256
BLK = 384
HALF = 48
BF, F32 = jnp.bfloat16, jnp.float32
SCALE = 1.4426950408889634 / (2.0 * F)


def place():
    r = lax.axis_index("row")
    c = lax.axis_index("col")
    return r % 4, r // 4, (c // 2) % 2, c // 4, c % 2


def device(x, l, h, z, k):
    return (l * 4 + x, z * 4 + h * 2 + k)


def both(*conds):
    out = conds[0]
    for cond in conds[1:]:
        out = jnp.logical_and(out, cond)
    return out


def dot_t(a, b):
    return lax.dot_general(a, b, (((1,), (1,)), ((), ())), preferred_element_type=F32)


def dot(a, b):
    return jnp.dot(a, b, preferred_element_type=F32)


def halves(a):
    high = a.astype(BF)
    return high, (a - high.astype(F32)).astype(BF)


def whiten(values, w_high, w_low):
    high, low = halves(values)
    return (dot(high, w_high) + dot(high, w_low) + dot(low, w_high)).astype(BF)


def square_sums(points):
    wide = points.astype(F32)
    return jnp.sum(wide * wide, axis=1, keepdims=True) * -SCALE


def as_row(column):
    n = column.shape[0]
    return jnp.transpose(jnp.broadcast_to(column, (n, 128)))[0:1, :]


def gaussian(left, right, left_sums, right_sums):
    return jnp.exp2((2.0 * SCALE) * dot_t(left, right) + (left_sums + right_sums))


def add_ridge(ref, span, gap):
    shape = (BLK, ref.shape[1])

    @pl.when(both(gap > -shape[1], gap < shape[0]))
    def _():
        i = lax.broadcasted_iota(jnp.int32, shape, 0)
        j = lax.broadcasted_iota(jnp.int32, shape, 1)
        ref[span, :] += jnp.where(i - j == gap, RIDGE, 0.0)


class Sender:
    def __init__(self, sems):
        self.sems = sems
        self.items = []

    def send(self, src, dst, recv, dev, cond=None):
        n = len(self.items)

        def make():
            return pltpu.make_async_remote_copy(
                src, dst, self.sems.at[n], recv, device_id=dev, device_id_type=MESH
            )

        self.items.append((make, cond))
        if cond is None:
            make().start()
        else:
            pl.when(cond)(lambda: make().start())

    def drain(self):
        for make, cond in self.items:
            if cond is None:
                make().wait_send()
            else:
                pl.when(cond)(lambda make=make: make().wait_send())


def arrived(ref, sem, cond=None):
    def wait():
        pltpu.make_async_copy(ref, ref, sem).wait()

    if cond is None:
        wait()
    else:
        pl.when(cond)(wait)


def main_kernel(
    x_in, coef_in, w_in, t_in,
    kern, res,
    pr, pc, xr, xc, xp, coef, w, t, top, sp, sj, wh, wl, k0, part, pbuf, ybuf, yrecv, sbuf, rbuf,
    ssem, za, yb, yc, sa, sb, sc, xps, xms, yx, op, om, op2, xsend, p1, p2, p3, loc, s1, s1s, s3, s3s, s2, s2s, s4, s4s,
):
    x, l, h, z, k = place()
    r = l * 4 + x
    c = z * 4 + h * 2 + k
    zplus, zminus = device(x, l, h, (z + 1) % 8, k), device(x, l, h, (z + 7) % 8, k)
    ypart, sib = device(x, l, 1 - h, z, k), device(x, l, h, z, 1 - k)
    xplus, xminus = device((x + 1) % 4, l, h, z, k), device((x + 3) % 4, l, h, z, k)
    yl = device(x, 1 - l, h, z, k)
    t_of_me = 4 * r + 2 * h + k
    is_owner = both(r == 0, c < 6)
    self_piece = both(r == 0, c == 0)
    not_self = jnp.logical_not(self_piece)
    is_place = z == jnp.where(t_of_me < 24, 0, 1)

    def first(p, hh, kk):
        return 384 * p + 96 * (2 * hh + kk)

    def rows(start, n):
        return xr.at[pl.ds(pl.multiple_of(start, 16), n)]

    own = first(z, h, k)
    fetches = [
        pltpu.make_async_copy(x_in, rows(own, 96), loc.at[0]),
        pltpu.make_async_copy(coef_in, coef, loc.at[1]),
        pltpu.make_async_copy(w_in, w, loc.at[2]),
        pltpu.make_async_copy(t_in, t, loc.at[3]),
    ]
    for fetch in fetches:
        fetch.start()

    bar = pltpu.get_barrier_semaphore()

    def hello(dev):
        pl.semaphore_signal(bar, inc=1, device_id=dev, device_id_type=MESH)

    for i in range(1, 16):
        hello(((r + i // 2) % 8, z * 4 + ((h + i) % 2) * 2 + k))
    for i in range(2, 16):
        hello(device(x, l, (h + i) % 2, (z + i // 2) % 8, k))
    hello(sib)
    pl.when(both(is_place, not_self))(lambda: hello((0, t_of_me // 6)))
    extra = jnp.where(c == 0, 5, jnp.where(c < 5, 6, 2))
    pl.semaphore_wait(bar, 30 + jnp.where(is_owner, extra, 0))

    out = Sender(ssem)

    def piece(p, n):
        return rows(first(p, h, k) + HALF * n if n < 2 else first(p, 1 - h, k), HALF)

    def plane(s, d):
        return (z + 16 - d * s) % 8

    def slot(s, n):
        return 0 if s == 0 else 2 * s - 1 + n

    first_copy = fetches[0]
    mine = [x_in.at[pl.ds(HALF * n, HALF)] for n in range(2)]
    out.send(mine[0], piece(z, 0), yb.at[0], ypart)
    for n in range(2):
        out.send(mine[n], piece(z, n), za.at[n], zplus)
        out.send(mine[n], piece(z, n), za.at[3 + n], zminus)
    out.send(mine[1], piece(z, 1), yc.at[0], ypart)
    out.send(x_in, rows(own, 96), sa.at[0], sib)
    arrived(piece(z, 2), yb.at[0])
    out.send(piece(z, 2), piece(z, 2), za.at[2], zplus)
    out.send(piece(z, 2), piece(z, 2), za.at[5], zminus)
    out.send(piece(z, 2), piece(z, 2), sb.at[0], sib)

    def late(s):
        pairs = [(n, d) for n, d in enumerate((1, -1)) if not (s in (0, 4) and n == 1)]
        for n, d in pairs:
            i, p = slot(s, n), plane(s, d)
            got = rows(first(p, 1 - h, k) + HALF, HALF)
            arrived(got, yc.at[i])
            out.send(got, got, sc.at[i], sib)
        for n, d in pairs:
            i, p = slot(s, n), plane(s, d)
            arrived(rows(first(p, h, 1 - k), 96), sa.at[i])
            arrived(rows(first(p, 1 - h, 1 - k), HALF), sb.at[i])
            arrived(rows(first(p, 1 - h, 1 - k) + HALF, HALF), sc.at[i])

    xs, ls = z % 4, z // 4
    q = (x + 4 - xs) % 4
    line = l == ls
    other = jnp.logical_not(line)
    hops_plus, hops_minus = q, (4 - q) % 4
    b0, bm, bp, bo = (q + 3) % 4, (q + 2) % 4, q, (q + 1) % 4

    def gap(j):
        away = (4 * h + 2 * k + j + 8 - z) % 8
        return jnp.minimum(away, 8 - away)

    def block(j, b, half=None):
        start = 384 * j + 96 * b + (0 if half is None else HALF * half)
        return xc.at[pl.ds(pl.multiple_of(start, 16), 96 if half is None else HALF)]

    def raw(j, b):
        return rows(384 * (4 * h + 2 * k + j) + 96 * b, 96)

    def remote(src, dst, n, recv, dev):
        return pltpu.make_async_remote_copy(src, dst, xsend.at[n], recv, device_id=dev, device_id_type=MESH)

    across = device((x + 2) % 4, l, h, z, k)
    yl_across = device((x + 2) % 4, 1 - l, h, z, k)

    def part_of(ref, n):
        return ref.at[pl.ds(HALF * n, HALF)]

    def column_stage(s):
        def step(j, carry):
            g = gap(j)

            @pl.when(both(line, q == 0, g == s))
            def _():
                remote(raw(j, 3), block(j, 3), 10 * j + 8, yx.at[j], yl).start()
                remote(raw(j, 1), block(j, 1), 10 * j + 9, yx.at[j], yl_across).start()
                for u in range(4):
                    b, half = u // 2, u % 2
                    remote(part_of(raw(j, b), half), block(j, b, half), 10 * j + u, xps.at[4 * j + u], xplus).start()
                    b = 2 + b
                    remote(part_of(raw(j, b), half), block(j, b, half), 10 * j + 4 + u, xms.at[4 * j + u], xminus).start()

            @pl.when(both(line, q != 0, g + hops_plus == s))
            def _():
                for u in range(4):
                    got = block(j, u // 2, u % 2)
                    arrived(got, xps.at[4 * j + u])
                    pl.when(q != 3)(lambda: remote(got, got, 10 * j + u, xps.at[4 * j + u], xplus).start())
                    if u == 1:
                        pl.when(q == 1)(lambda: remote(block(j, 0), block(j, 0), 10 * j + 8, yx.at[j], yl).start())

            @pl.when(both(line, q != 0, g + hops_minus == s))
            def _():
                for u in range(4):
                    got = block(j, 2 + u // 2, u % 2)
                    arrived(got, xms.at[4 * j + u])
                    pl.when(q != 1)(lambda: remote(got, got, 10 * j + 4 + u, xms.at[4 * j + u], xminus).start())
                    if u == 1:
                        pl.when(q == 3)(lambda: remote(block(j, 2), block(j, 2), 10 * j + 8, yx.at[j], yl).start())

            @pl.when(both(other, g + 1 + q % 2 == s))
            def _():
                got = block(j, b0)
                arrived(got, yx.at[j])
                remote(got, got, 10 * j, op.at[j], xplus).start()
                remote(got, got, 10 * j + 1, om.at[j], xminus).start()
                remote(got, got, 10 * j + 2, op2.at[j], across).start()

            return carry

        lax.fori_loop(0, 2, step, 0)

    def columns_end():
        def step(j, carry):
            @pl.when(other)
            def _():
                arrived(block(j, bm), op.at[j])
                arrived(block(j, bp), om.at[j])
                arrived(block(j, bo), op2.at[j])
                for n in range(3):
                    remote(block(j, 0), block(j, 0), 10 * j + n, op.at[0], xplus).wait_send()

            for u in range(4):
                piece_of = block(j, 0, 0)
                pl.when(both(line, q != 3))(lambda: remote(piece_of, piece_of, 10 * j + u, xps.at[0], xplus).wait_send())
                pl.when(both(line, q != 1))(lambda: remote(piece_of, piece_of, 10 * j + 4 + u, xms.at[0], xminus).wait_send())
            pl.when(both(line, q != 2))(lambda: remote(block(j, 0), block(j, 0), 10 * j + 8, yx.at[0], yl).wait_send())
            pl.when(both(line, q == 0))(lambda: remote(block(j, 0), block(j, 0), 10 * j + 9, yx.at[0], yl).wait_send())
            return carry

        lax.fori_loop(0, 2, step, 0)

    def panel_points_out():
        for j in range(6):
            tt = 6 * c + j
            has = both(is_owner, tt < 32)
            out.send(
                x_in.at[pl.ds(16 * j, 16)],
                xp.at[tt // 4, (tt // 2) % 2, tt % 2],
                p1.at[0],
                (tt // 4, jnp.where(tt < 24, 0, 4) + tt % 4),
                both(has, tt > 0) if j == 0 else has,
            )

        @pl.when(self_piece)
        def _():
            keep = pltpu.make_async_copy(x_in.at[pl.ds(0, 16)], xp.at[0, 0, 0], loc.at[4])
            keep.start()
            keep.wait()

    def panel_points_planes():
        got = xp.at[r, h, k]
        arrived(got, p1.at[0], both(is_place, not_self))
        for i in range(1, 8):
            out.send(got, got, p1.at[0], device(x, l, h, (z + i) % 8, k), is_place)

    def panel_points_plane():
        got = xp.at[r, h, k]
        arrived(got, p1.at[0], jnp.logical_not(is_place))
        for i in range(1, 16):
            out.send(got, got, p2.at[i - 1], ((r + i // 2) % 8, z * 4 + ((h + i) % 2) * 2 + k))

    def panel_points_chip():
        for i in range(1, 16):
            arrived(xp.at[(r + 8 - i // 2) % 8, (h + i) % 2, k], p2.at[i - 1])
        got = xp.at[:, :, k]
        out.send(got, got, p3.at[0], sib)

    for s in range(1, 5):
        if s < 4:
            for n in range(3):
                for e, d in enumerate((1, -1)):
                    got = piece(plane(s, d), n)
                    i = slot(s, e)
                    arrived(got, za.at[6 * (s - 1) + 3 * e + n])
                    if s < 3:
                        out.send(got, got, za.at[6 * s + 3 * e + n], zplus if d == 1 else zminus)
                    if n == 1:
                        out.send(got, got, yc.at[i], ypart)
                        whole = rows(first(plane(s, d), h, k), 96)
                        out.send(whole, whole, sa.at[i], sib)
                    if n == 2:
                        out.send(got, got, sb.at[i], sib)
                if s == 3:
                    d = (1 - 2 * k) if n < 2 else (2 * k - 1)
                    got = piece((z + 16 - 3 * d) % 8, n)
                    out.send(got, got, za.at[18 + n], device(x, l, h, (z + 8 + d) % 8, k))
        else:
            for n in range(3):
                got = piece(plane(4, 1), n)
                arrived(got, za.at[18 + n])
                if n == 1:
                    out.send(got, got, yc.at[7], ypart)
                    whole = rows(first(plane(4, 1), h, k), 96)
                    out.send(whole, whole, sa.at[7], sib)
                if n == 2:
                    out.send(got, got, sb.at[7], sib)
        if s == 1:
            panel_points_out()
            first_copy.wait()
        if s == 2:
            panel_points_planes()
        late(s - 1)
        column_stage(s - 1)
    panel_points_plane()
    late(4)
    keep = pltpu.make_async_copy(rows(768 * (2 * h + k), 768), xc, loc.at[4])
    source = both(line, q == 0)
    column_stage(4)
    pl.when(source)(lambda: keep.start())
    for fetch in fetches[1:]:
        fetch.wait()
    for i in range(2):
        high, low = halves(w[i])
        wh[i] = high
        wl[i] = low
    panel_points_chip()
    row_first = r * ROWS
    col_first = c * COLS
    heads = xp.reshape(2 * PANEL, F)

    def panels(points, start):
        k0[...] = gaussian(points, heads[...], square_sums(points), sp[...])
        add_ridge(k0, pl.ds(0, BLK), -start)
        p1 = whiten(k0[:, :PANEL], wh[0], wl[0])
        return p1, whiten(k0[:, PANEL:] - dot_t(p1, top[...]), wh[1], wl[1])

    def panel_rows(b):
        span = pl.ds(pl.multiple_of(b * BLK, BLK), BLK)
        p1, p2 = panels(xr[span, :], row_first + b * BLK)
        pr[span, :PANEL] = p1
        pr[span, PANEL:] = p2

    column_stage(5)
    column_stage(6)
    arrived(xp.at[:, :, 1 - k], p3.at[0])
    sp[...] = as_row(square_sums(heads[...]))
    lower = heads[PANEL:, :]
    top[...] = whiten(gaussian(lower, heads[:PANEL, :], square_sums(lower), sp[:, :PANEL]), wh[0], wl[0])

    def panel_copy(b):
        rows_of = pr.at[pl.ds(pl.multiple_of(b * BLK, BLK), BLK)]
        return pltpu.make_async_remote_copy(
            rows_of, rows_of, s4s.at[b // 2], s4.at[b // 2], device_id=sib, device_id_type=MESH
        )

    def my_panels(n, carry):
        pl.when(n >= 1)(lambda: panel_copy(2 * n - 2 + k).start())
        panel_rows(2 * n + k)
        return carry

    lax.fori_loop(0, 4, my_panels, 0)
    column_stage(7)
    panel_copy(6 + k).start()
    pl.when(source)(lambda: keep.wait())
    columns_end()

    sj[...] = as_row(square_sums(xc[...]))
    def turn(i):
        return (4 + ((i + 1) // 2) * (2 * (i % 2) - 1)) % 8

    def to_sib(i):
        zz = (z + turn(i)) % 8
        return pltpu.make_async_remote_copy(
            part.at[zz, :, 1 - k], pbuf.at[zz], s1s.at[i], s1.at[i], device_id=sib, device_id_type=MESH
        )

    def to_pair(i):
        zz = (z + turn(i)) % 8
        return pltpu.make_async_remote_copy(
            ybuf.at[zz], yrecv.at[zz], s3s.at[i], s3.at[i], device_id=ypart, device_id_type=MESH
        )

    def to_owner(i):
        d = turn(i)
        return pltpu.make_async_remote_copy(
            sbuf.at[d], rbuf.at[d], s2s.at[d], s2.at[d], device_id=device(x, l, h, (z + d) % 8, k), device_id_type=MESH
        )

    def exchange(i):
        @pl.when(both(i >= 1, i < 9))
        def _():
            to_sib(i - 1).start()

        @pl.when(both(i >= 3, i < 11))
        def _():
            to_pair(i - 3).start()

        @pl.when(both(i >= 6, i < 13))
        def _():
            to_owner(i - 6).start()

    def chip_sum(i):
        @pl.when(both(i >= 2, i < 10))
        def _():
            zz = (z + turn(i - 2)) % 8
            arrived(pbuf.at[zz], s1.at[i - 2])
            ybuf[zz] = (part[zz, 1 - h, k] + pbuf[zz, 1 - h]).astype(BF)

        @pl.when(both(i >= 5, i < 13))
        def _():
            d = turn(i - 5)
            zz = (z + d) % 8
            arrived(yrecv.at[zz], s3.at[i - 5])
            sbuf[d] = (part[zz, h, k] + pbuf[zz, h] + yrecv[zz].astype(F32)).astype(BF)

    def span_of(i):
        return pl.ds(pl.multiple_of((z + turn(i)) % 8 * BLK, BLK), BLK)

    def values(i):
        span = span_of(i)
        points = xr[span, :]
        kern[span, :] = gaussian(points, xc[...], square_sums(points), sj[...])

    def ridge(i):
        add_ridge(kern, span_of(i), col_first - row_first - (z + turn(i)) % 8 * BLK)

    def products(i):
        part[(z + turn(i)) % 8] = dot(kern[span_of(i), :].astype(BF), coef[...]).reshape(2, 2, SHARD, NRESP)

    values(0)
    ridge(0)

    def tile_step(i, carry):
        exchange(i - 1)
        products(i - 1)
        values(i)
        ridge(i)
        chip_sum(i - 1)
        return carry

    lax.fori_loop(1, 8, tile_step, 0)
    exchange(7)
    products(7)
    chip_sum(7)

    def panel_cols(j, carry):
        span = pl.ds(pl.multiple_of(j * BLK, BLK), BLK)
        exchange(j + 8)
        p1, p2 = panels(xc[span, :], col_first + j * BLK)
        pc[span, :PANEL] = p1
        pc[span, PANEL:] = p2
        chip_sum(j + 8)
        return carry

    lax.fori_loop(0, 2, panel_cols, 0)

    def update_step(b, carry):
        exchange(b + 10)
        span = pl.ds(pl.multiple_of(b * BLK, BLK), BLK)
        kern[span, :] -= dot_t(pr[span, :], pc[...])
        chip_sum(b + 10)
        return carry

    for n in range(4):
        panel_copy(2 * n + 1 - k).wait_recv()
        panel_copy(2 * n + k).wait_send()
    lax.fori_loop(0, 8, update_step, 0)

    acc = t[...] - sbuf[0].astype(F32)
    for d in (1, 7, 2, 6, 3, 5, 4):
        arrived(rbuf.at[d], s2.at[d])
        acc = acc - rbuf[d].astype(F32)
    res[...] = acc
    for i in range(8):
        to_sib(i).wait_send()
        to_pair(i).wait_send()
        if i < 7:
            to_owner(i).wait_send()
    out.drain()


def store_kernel(kern, upd, sem):
    copies = [pltpu.make_async_copy(kern.at[pl.ds(BLK * b, BLK)], upd.at[pl.ds(BLK * b, BLK)], sem.at[b]) for b in range(8)]
    for copy in copies:
        copy.start()
    for copy in copies:
        copy.wait()


def body(descriptors, coefficients, targets, whitening):
    dma = pltpu.SemaphoreType.DMA
    vm = pl.BlockSpec(memory_space=pltpu.VMEM)
    hbm = pl.BlockSpec(memory_space=pltpu.HBM)
    V = pltpu.VMEM
    kern, residual = pl.pallas_call(
        main_kernel,
        out_shape=(
            jax.ShapeDtypeStruct((ROWS, COLS), F32),
            jax.ShapeDtypeStruct((SHARD, NRESP), F32),
        ),
        in_specs=[hbm] * 4,
        out_specs=(vm, vm),
        scratch_shapes=[
            V((ROWS, 2 * PANEL), BF), V((COLS, 2 * PANEL), BF), V((ROWS, F), BF), V((COLS, F), BF), V((8, 2, 2, 16, F), BF), V((COLS, NRESP), BF), V((2, PANEL, PANEL), F32),
            V((SHARD, NRESP), F32), V((PANEL, PANEL), BF), V((1, 2 * PANEL), F32), V((1, COLS), F32),
            V((2, PANEL, PANEL), BF), V((2, PANEL, PANEL), BF), V((BLK, 2 * PANEL), F32), V((8, 2, 2, SHARD, NRESP), F32),
            V((8, 2, SHARD, NRESP), F32), V((8, SHARD, NRESP), BF), V((8, SHARD, NRESP), BF),
            V((8, SHARD, NRESP), BF), V((8, SHARD, NRESP), BF),
            dma((180,)), dma((21,)), dma((1,)), dma((8,)), dma((8,)), dma((8,)), dma((8,)), dma((8,)), dma((8,)), dma((2,)),
            dma((2,)), dma((2,)), dma((2,)), dma((20,)), dma((1,)), dma((15,)), dma((1,)), dma((5,)),
            dma((8,)), dma((8,)), dma((8,)), dma((8,)), dma((8,)), dma((8,)), dma((4,)), dma((4,)),
        ],
        compiler_params=pltpu.CompilerParams(collective_id=0, has_side_effects=True, vmem_limit_bytes=32 << 20),
        name="main",
    )(*[pltpu.with_memory_space_constraint(a, pltpu.HBM) for a in (descriptors, coefficients, whitening, targets)])
    updated = pl.pallas_call(
        store_kernel,
        out_shape=jax.ShapeDtypeStruct((ROWS, COLS), F32),
        in_specs=[vm],
        out_specs=hbm,
        scratch_shapes=[dma((8,))],
        compiler_params=pltpu.CompilerParams(vmem_limit_bytes=16 << 20),
        name="store",
    )(kern)
    return updated, residual


def solution(mesh):
    in_specs = (P(("row", "col"), None), P("col", None), P(("row", "col"), None), P())
    out_specs = (P("row", "col"), P(("row", "col"), None))
    return jax.shard_map(body, mesh=mesh, in_specs=in_specs, out_specs=out_specs, check_vma=False)
```

```python
import jax
import jax.numpy as jnp
from jax import lax
from jax.experimental import pallas as pl
from jax.experimental.pallas import tpu as pltpu
from jax.sharding import PartitionSpec as P

MESH = pl.DeviceIdType.MESH
SHARD, F = 96, 768
ROWS, COLS = 3072, 768
RIDGE = 0.5
NRESP = 256
PANEL = 256
BLK = 384
HALF = 48
TAIL_BLOCKS = 2
BF, F32 = jnp.bfloat16, jnp.float32
SCALE = 1.4426950408889634 / (2.0 * F)


def place():
    r = lax.axis_index("row")
    c = lax.axis_index("col")
    return r % 4, r // 4, (c // 2) % 2, c // 4, c % 2


def device(x, l, h, z, k):
    return (l * 4 + x, z * 4 + h * 2 + k)


def both(*conds):
    out = conds[0]
    for cond in conds[1:]:
        out = jnp.logical_and(out, cond)
    return out


def dot_t(a, b):
    return lax.dot_general(a, b, (((1,), (1,)), ((), ())), preferred_element_type=F32)


def dot(a, b):
    return jnp.dot(a, b, preferred_element_type=F32)


def halves(a):
    high = a.astype(BF)
    return high, (a - high.astype(F32)).astype(BF)


def whiten(values, w_high, w_low):
    high, low = halves(values)
    return (dot(high, w_high) + dot(high, w_low) + dot(low, w_high)).astype(BF)


def square_sums(points):
    wide = points.astype(F32)
    return jnp.sum(wide * wide, axis=1, keepdims=True) * -SCALE


def as_row(column):
    n = column.shape[0]
    return jnp.transpose(jnp.broadcast_to(column, (n, 128)))[0:1, :]


def gaussian(left, right, left_sums, right_sums):
    return jnp.exp2((2.0 * SCALE) * dot_t(left, right) + (left_sums + right_sums))


def add_ridge(ref, span, gap):
    shape = (BLK, ref.shape[1])

    @pl.when(both(gap > -shape[1], gap < shape[0]))
    def _():
        i = lax.broadcasted_iota(jnp.int32, shape, 0)
        j = lax.broadcasted_iota(jnp.int32, shape, 1)
        ref[span, :] += jnp.where(i - j == gap, RIDGE, 0.0)


class Sender:
    def __init__(self, sems):
        self.sems = sems
        self.items = []

    def send(self, src, dst, recv, dev, cond=None):
        n = len(self.items)

        def make():
            return pltpu.make_async_remote_copy(
                src, dst, self.sems.at[n], recv, device_id=dev, device_id_type=MESH
            )

        self.items.append((make, cond))
        if cond is None:
            make().start()
        else:
            pl.when(cond)(lambda: make().start())

    def drain(self):
        for make, cond in self.items:
            if cond is None:
                make().wait_send()
            else:
                pl.when(cond)(lambda make=make: make().wait_send())


def arrived(ref, sem, cond=None):
    def wait():
        pltpu.make_async_copy(ref, ref, sem).wait()

    if cond is None:
        wait()
    else:
        pl.when(cond)(wait)


def main_kernel(
    x_in, coef_in, w_in, t_in,
    kern, res,
    pr, pc, xr, xc, xp, coef, w, t, top, sp, sj, wh, wl, k0, part, pbuf, ybuf, yrecv, sbuf, rbuf,
    ssem, za, yb, yc, sa, sb, sc, xps, xms, yx, op, om, op2, xsend, p1, p2, p3, loc, s1, s1s, s3, s3s, s2, s2s, s4, s4s,
):
    x, l, h, z, k = place()
    r = l * 4 + x
    c = z * 4 + h * 2 + k
    zplus, zminus = device(x, l, h, (z + 1) % 8, k), device(x, l, h, (z + 7) % 8, k)
    ypart, sib = device(x, l, 1 - h, z, k), device(x, l, h, z, 1 - k)
    xplus, xminus = device((x + 1) % 4, l, h, z, k), device((x + 3) % 4, l, h, z, k)
    yl = device(x, 1 - l, h, z, k)
    t_of_me = 4 * r + 2 * h + k
    is_owner = both(r == 0, c < 6)
    self_piece = both(r == 0, c == 0)
    not_self = jnp.logical_not(self_piece)
    is_place = z == jnp.where(t_of_me < 24, 0, 1)

    def first(p, hh, kk):
        return 384 * p + 96 * (2 * hh + kk)

    def rows(start, n):
        return xr.at[pl.ds(pl.multiple_of(start, 16), n)]

    own = first(z, h, k)
    fetches = [
        pltpu.make_async_copy(x_in, rows(own, 96), loc.at[0]),
        pltpu.make_async_copy(coef_in, coef, loc.at[1]),
        pltpu.make_async_copy(w_in, w, loc.at[2]),
        pltpu.make_async_copy(t_in, t, loc.at[3]),
    ]
    for fetch in fetches:
        fetch.start()

    bar = pltpu.get_barrier_semaphore()

    def hello(dev):
        pl.semaphore_signal(bar, inc=1, device_id=dev, device_id_type=MESH)

    for i in range(1, 16):
        hello(((r + i // 2) % 8, z * 4 + ((h + i) % 2) * 2 + k))
    for i in range(2, 16):
        hello(device(x, l, (h + i) % 2, (z + i // 2) % 8, k))
    hello(sib)
    pl.when(both(is_place, not_self))(lambda: hello((0, t_of_me // 6)))
    extra = jnp.where(c == 0, 5, jnp.where(c < 5, 6, 2))
    pl.semaphore_wait(bar, 30 + jnp.where(is_owner, extra, 0))

    out = Sender(ssem)

    def piece(p, n):
        return rows(first(p, h, k) + HALF * n if n < 2 else first(p, 1 - h, k), HALF)

    def plane(s, d):
        return (z + 16 - d * s) % 8

    def slot(s, n):
        return 0 if s == 0 else 2 * s - 1 + n

    first_copy = fetches[0]
    mine = [x_in.at[pl.ds(HALF * n, HALF)] for n in range(2)]
    out.send(mine[0], piece(z, 0), yb.at[0], ypart)
    for n in range(2):
        out.send(mine[n], piece(z, n), za.at[n], zplus)
        out.send(mine[n], piece(z, n), za.at[3 + n], zminus)
    out.send(mine[1], piece(z, 1), yc.at[0], ypart)
    out.send(x_in, rows(own, 96), sa.at[0], sib)
    arrived(piece(z, 2), yb.at[0])
    out.send(piece(z, 2), piece(z, 2), za.at[2], zplus)
    out.send(piece(z, 2), piece(z, 2), za.at[5], zminus)
    out.send(piece(z, 2), piece(z, 2), sb.at[0], sib)

    def late(s):
        pairs = [(n, d) for n, d in enumerate((1, -1)) if not (s in (0, 4) and n == 1)]
        for n, d in pairs:
            i, p = slot(s, n), plane(s, d)
            got = rows(first(p, 1 - h, k) + HALF, HALF)
            arrived(got, yc.at[i])
            out.send(got, got, sc.at[i], sib)
        for n, d in pairs:
            i, p = slot(s, n), plane(s, d)
            arrived(rows(first(p, h, 1 - k), 96), sa.at[i])
            arrived(rows(first(p, 1 - h, 1 - k), HALF), sb.at[i])
            arrived(rows(first(p, 1 - h, 1 - k) + HALF, HALF), sc.at[i])

    xs, ls = z % 4, z // 4
    q = (x + 4 - xs) % 4
    line = l == ls
    other = jnp.logical_not(line)
    hops_plus, hops_minus = q, (4 - q) % 4
    b0, bm, bp, bo = (q + 3) % 4, (q + 2) % 4, q, (q + 1) % 4

    def gap(j):
        away = (4 * h + 2 * k + j + 8 - z) % 8
        return jnp.minimum(away, 8 - away)

    def block(j, b, half=None):
        start = 384 * j + 96 * b + (0 if half is None else HALF * half)
        return xc.at[pl.ds(pl.multiple_of(start, 16), 96 if half is None else HALF)]

    def raw(j, b):
        return rows(384 * (4 * h + 2 * k + j) + 96 * b, 96)

    def remote(src, dst, n, recv, dev):
        return pltpu.make_async_remote_copy(src, dst, xsend.at[n], recv, device_id=dev, device_id_type=MESH)

    across = device((x + 2) % 4, l, h, z, k)
    yl_across = device((x + 2) % 4, 1 - l, h, z, k)

    def part_of(ref, n):
        return ref.at[pl.ds(HALF * n, HALF)]

    def column_stage(s):
        def step(j, carry):
            g = gap(j)

            @pl.when(both(line, q == 0, g == s))
            def _():
                remote(raw(j, 3), block(j, 3), 10 * j + 8, yx.at[j], yl).start()
                remote(raw(j, 1), block(j, 1), 10 * j + 9, yx.at[j], yl_across).start()
                for u in range(4):
                    b, half = u // 2, u % 2
                    remote(part_of(raw(j, b), half), block(j, b, half), 10 * j + u, xps.at[4 * j + u], xplus).start()
                    b = 2 + b
                    remote(part_of(raw(j, b), half), block(j, b, half), 10 * j + 4 + u, xms.at[4 * j + u], xminus).start()

            @pl.when(both(line, q != 0, g + hops_plus == s))
            def _():
                for u in range(4):
                    got = block(j, u // 2, u % 2)
                    arrived(got, xps.at[4 * j + u])
                    pl.when(q != 3)(lambda: remote(got, got, 10 * j + u, xps.at[4 * j + u], xplus).start())
                    if u == 1:
                        pl.when(q == 1)(lambda: remote(block(j, 0), block(j, 0), 10 * j + 8, yx.at[j], yl).start())

            @pl.when(both(line, q != 0, g + hops_minus == s))
            def _():
                for u in range(4):
                    got = block(j, 2 + u // 2, u % 2)
                    arrived(got, xms.at[4 * j + u])
                    pl.when(q != 1)(lambda: remote(got, got, 10 * j + 4 + u, xms.at[4 * j + u], xminus).start())
                    if u == 1:
                        pl.when(q == 3)(lambda: remote(block(j, 2), block(j, 2), 10 * j + 8, yx.at[j], yl).start())

            @pl.when(both(other, g + 1 + q % 2 == s))
            def _():
                got = block(j, b0)
                arrived(got, yx.at[j])
                remote(got, got, 10 * j, op.at[j], xplus).start()
                remote(got, got, 10 * j + 1, om.at[j], xminus).start()
                remote(got, got, 10 * j + 2, op2.at[j], across).start()

            return carry

        lax.fori_loop(0, 2, step, 0)

    def columns_end():
        def step(j, carry):
            @pl.when(other)
            def _():
                arrived(block(j, bm), op.at[j])
                arrived(block(j, bp), om.at[j])
                arrived(block(j, bo), op2.at[j])
                for n in range(3):
                    remote(block(j, 0), block(j, 0), 10 * j + n, op.at[0], xplus).wait_send()

            for u in range(4):
                piece_of = block(j, 0, 0)
                pl.when(both(line, q != 3))(lambda: remote(piece_of, piece_of, 10 * j + u, xps.at[0], xplus).wait_send())
                pl.when(both(line, q != 1))(lambda: remote(piece_of, piece_of, 10 * j + 4 + u, xms.at[0], xminus).wait_send())
            pl.when(both(line, q != 2))(lambda: remote(block(j, 0), block(j, 0), 10 * j + 8, yx.at[0], yl).wait_send())
            pl.when(both(line, q == 0))(lambda: remote(block(j, 0), block(j, 0), 10 * j + 9, yx.at[0], yl).wait_send())
            return carry

        lax.fori_loop(0, 2, step, 0)

    def panel_points_out():
        for j in range(6):
            tt = 6 * c + j
            has = both(is_owner, tt < 32)
            out.send(
                x_in.at[pl.ds(16 * j, 16)],
                xp.at[tt // 4, (tt // 2) % 2, tt % 2],
                p1.at[0],
                (tt // 4, jnp.where(tt < 24, 0, 4) + tt % 4),
                both(has, tt > 0) if j == 0 else has,
            )

        @pl.when(self_piece)
        def _():
            keep = pltpu.make_async_copy(x_in.at[pl.ds(0, 16)], xp.at[0, 0, 0], loc.at[4])
            keep.start()
            keep.wait()

    def panel_points_planes():
        got = xp.at[r, h, k]
        arrived(got, p1.at[0], both(is_place, not_self))
        for i in range(1, 8):
            out.send(got, got, p1.at[0], device(x, l, h, (z + i) % 8, k), is_place)

    def panel_points_plane():
        got = xp.at[r, h, k]
        arrived(got, p1.at[0], jnp.logical_not(is_place))
        for i in range(1, 16):
            out.send(got, got, p2.at[i - 1], ((r + i // 2) % 8, z * 4 + ((h + i) % 2) * 2 + k))

    def panel_points_chip():
        for i in range(1, 16):
            arrived(xp.at[(r + 8 - i // 2) % 8, (h + i) % 2, k], p2.at[i - 1])
        got = xp.at[:, :, k]
        out.send(got, got, p3.at[0], sib)

    for s in range(1, 5):
        if s < 4:
            for n in range(3):
                for e, d in enumerate((1, -1)):
                    got = piece(plane(s, d), n)
                    i = slot(s, e)
                    arrived(got, za.at[6 * (s - 1) + 3 * e + n])
                    if s < 3:
                        out.send(got, got, za.at[6 * s + 3 * e + n], zplus if d == 1 else zminus)
                    if n == 1:
                        out.send(got, got, yc.at[i], ypart)
                        whole = rows(first(plane(s, d), h, k), 96)
                        out.send(whole, whole, sa.at[i], sib)
                    if n == 2:
                        out.send(got, got, sb.at[i], sib)
                if s == 3:
                    d = (1 - 2 * k) if n < 2 else (2 * k - 1)
                    got = piece((z + 16 - 3 * d) % 8, n)
                    out.send(got, got, za.at[18 + n], device(x, l, h, (z + 8 + d) % 8, k))
        else:
            for n in range(3):
                got = piece(plane(4, 1), n)
                arrived(got, za.at[18 + n])
                if n == 1:
                    out.send(got, got, yc.at[7], ypart)
                    whole = rows(first(plane(4, 1), h, k), 96)
                    out.send(whole, whole, sa.at[7], sib)
                if n == 2:
                    out.send(got, got, sb.at[7], sib)
        if s == 1:
            panel_points_out()
            first_copy.wait()
        if s == 2:
            panel_points_planes()
        late(s - 1)
        column_stage(s - 1)
    panel_points_plane()
    late(4)
    keep = pltpu.make_async_copy(rows(768 * (2 * h + k), 768), xc, loc.at[4])
    source = both(line, q == 0)
    column_stage(4)
    pl.when(source)(lambda: keep.start())
    for fetch in fetches[1:]:
        fetch.wait()
    for i in range(2):
        high, low = halves(w[i])
        wh[i] = high
        wl[i] = low
    panel_points_chip()
    row_first = r * ROWS
    col_first = c * COLS
    heads = xp.reshape(2 * PANEL, F)

    def panels(points, start):
        k0[...] = gaussian(points, heads[...], square_sums(points), sp[...])
        add_ridge(k0, pl.ds(0, BLK), -start)
        p1 = whiten(k0[:, :PANEL], wh[0], wl[0])
        return p1, whiten(k0[:, PANEL:] - dot_t(p1, top[...]), wh[1], wl[1])

    def panel_rows(b):
        span = pl.ds(pl.multiple_of(b * BLK, BLK), BLK)
        p1, p2 = panels(xr[span, :], row_first + b * BLK)
        pr[span, :PANEL] = p1
        pr[span, PANEL:] = p2

    column_stage(5)
    column_stage(6)
    arrived(xp.at[:, :, 1 - k], p3.at[0])
    sp[...] = as_row(square_sums(heads[...]))
    lower = heads[PANEL:, :]
    top[...] = whiten(gaussian(lower, heads[:PANEL, :], square_sums(lower), sp[:, :PANEL]), wh[0], wl[0])

    def panel_copy(b):
        rows_of = pr.at[pl.ds(pl.multiple_of(b * BLK, BLK), BLK)]
        return pltpu.make_async_remote_copy(
            rows_of, rows_of, s4s.at[b // 2], s4.at[b // 2], device_id=sib, device_id_type=MESH
        )

    def my_panels(n, carry):
        pl.when(n >= 1)(lambda: panel_copy(2 * n - 2 + k).start())
        panel_rows(2 * n + k)
        return carry

    lax.fori_loop(0, TAIL_BLOCKS, my_panels, 0)
    column_stage(7)
    pl.when(source)(lambda: keep.wait())
    columns_end()

    sj[...] = as_row(square_sums(xc[...]))
    def turn(i):
        return (4 + ((i + 1) // 2) * (2 * (i % 2) - 1)) % 8

    def to_sib(i):
        zz = (z + turn(i)) % 8
        return pltpu.make_async_remote_copy(
            part.at[zz, :, 1 - k], pbuf.at[zz], s1s.at[i], s1.at[i], device_id=sib, device_id_type=MESH
        )

    def to_pair(i):
        zz = (z + turn(i)) % 8
        return pltpu.make_async_remote_copy(
            ybuf.at[zz], yrecv.at[zz], s3s.at[i], s3.at[i], device_id=ypart, device_id_type=MESH
        )

    def to_owner(i):
        d = turn(i)
        return pltpu.make_async_remote_copy(
            sbuf.at[d], rbuf.at[d], s2s.at[d], s2.at[d], device_id=device(x, l, h, (z + d) % 8, k), device_id_type=MESH
        )

    def exchange(i):
        @pl.when(both(i >= 1, i < 9))
        def _():
            to_sib(i - 1).start()

        @pl.when(both(i >= 3, i < 11))
        def _():
            to_pair(i - 3).start()

        @pl.when(both(i >= 6, i < 13))
        def _():
            to_owner(i - 6).start()

    def chip_sum(i):
        @pl.when(both(i >= 2, i < 10))
        def _():
            zz = (z + turn(i - 2)) % 8
            arrived(pbuf.at[zz], s1.at[i - 2])
            ybuf[zz] = (part[zz, 1 - h, k] + pbuf[zz, 1 - h]).astype(BF)

        @pl.when(both(i >= 5, i < 13))
        def _():
            d = turn(i - 5)
            zz = (z + d) % 8
            arrived(yrecv.at[zz], s3.at[i - 5])
            sbuf[d] = (part[zz, h, k] + pbuf[zz, h] + yrecv[zz].astype(F32)).astype(BF)

    def span_of(i):
        return pl.ds(pl.multiple_of((z + turn(i)) % 8 * BLK, BLK), BLK)

    def values(i):
        span = span_of(i)
        points = xr[span, :]
        kern[span, :] = gaussian(points, xc[...], square_sums(points), sj[...])

    def ridge(i):
        add_ridge(kern, span_of(i), col_first - row_first - (z + turn(i)) % 8 * BLK)

    def products(i):
        part[(z + turn(i)) % 8] = dot(kern[span_of(i), :].astype(BF), coef[...]).reshape(2, 2, SHARD, NRESP)

    values(0)
    ridge(0)

    def tile_step(i, carry):
        exchange(i - 1)
        products(i - 1)
        values(i)
        ridge(i)
        chip_sum(i - 1)
        return carry

    lax.fori_loop(1, 8, tile_step, 0)
    exchange(7)
    products(7)
    chip_sum(7)

    def more_panels(n, carry):
        exchange(n + 8 - TAIL_BLOCKS)
        my_panels(n, carry)
        chip_sum(n + 8 - TAIL_BLOCKS)
        return carry

    lax.fori_loop(TAIL_BLOCKS, 4, more_panels, 0)

    def panel_cols(j, carry):
        pl.when(j == 1)(lambda: panel_copy(6 + k).start())
        span = pl.ds(pl.multiple_of(j * BLK, BLK), BLK)
        exchange(j + 12 - TAIL_BLOCKS)
        p1, p2 = panels(xc[span, :], col_first + j * BLK)
        pc[span, :PANEL] = p1
        pc[span, PANEL:] = p2
        chip_sum(j + 12 - TAIL_BLOCKS)
        return carry

    lax.fori_loop(0, 2, panel_cols, 0)

    def update_step(b, carry):
        exchange(b + 14 - TAIL_BLOCKS)
        span = pl.ds(pl.multiple_of(b * BLK, BLK), BLK)
        kern[span, :] -= dot_t(pr[span, :], pc[...])
        chip_sum(b + 14 - TAIL_BLOCKS)
        return carry

    for n in range(4):
        panel_copy(2 * n + 1 - k).wait_recv()
        panel_copy(2 * n + k).wait_send()
    lax.fori_loop(0, 8, update_step, 0)

    acc = t[...] - sbuf[0].astype(F32)
    for d in (1, 7, 2, 6, 3, 5, 4):
        arrived(rbuf.at[d], s2.at[d])
        acc = acc - rbuf[d].astype(F32)
    res[...] = acc
    for i in range(8):
        to_sib(i).wait_send()
        to_pair(i).wait_send()
        if i < 7:
            to_owner(i).wait_send()
    out.drain()


def store_kernel(kern, upd, sem):
    copies = [pltpu.make_async_copy(kern.at[pl.ds(BLK * b, BLK)], upd.at[pl.ds(BLK * b, BLK)], sem.at[b]) for b in range(8)]
    for copy in copies:
        copy.start()
    for copy in copies:
        copy.wait()


def body(descriptors, coefficients, targets, whitening):
    dma = pltpu.SemaphoreType.DMA
    vm = pl.BlockSpec(memory_space=pltpu.VMEM)
    hbm = pl.BlockSpec(memory_space=pltpu.HBM)
    V = pltpu.VMEM
    kern, residual = pl.pallas_call(
        main_kernel,
        out_shape=(
            jax.ShapeDtypeStruct((ROWS, COLS), F32),
            jax.ShapeDtypeStruct((SHARD, NRESP), F32),
        ),
        in_specs=[hbm] * 4,
        out_specs=(vm, vm),
        scratch_shapes=[
            V((ROWS, 2 * PANEL), BF), V((COLS, 2 * PANEL), BF), V((ROWS, F), BF), V((COLS, F), BF), V((8, 2, 2, 16, F), BF), V((COLS, NRESP), BF), V((2, PANEL, PANEL), F32),
            V((SHARD, NRESP), F32), V((PANEL, PANEL), BF), V((1, 2 * PANEL), F32), V((1, COLS), F32),
            V((2, PANEL, PANEL), BF), V((2, PANEL, PANEL), BF), V((BLK, 2 * PANEL), F32), V((8, 2, 2, SHARD, NRESP), F32),
            V((8, 2, SHARD, NRESP), F32), V((8, SHARD, NRESP), BF), V((8, SHARD, NRESP), BF),
            V((8, SHARD, NRESP), BF), V((8, SHARD, NRESP), BF),
            dma((180,)), dma((21,)), dma((1,)), dma((8,)), dma((8,)), dma((8,)), dma((8,)), dma((8,)), dma((8,)), dma((2,)),
            dma((2,)), dma((2,)), dma((2,)), dma((20,)), dma((1,)), dma((15,)), dma((1,)), dma((5,)),
            dma((8,)), dma((8,)), dma((8,)), dma((8,)), dma((8,)), dma((8,)), dma((4,)), dma((4,)),
        ],
        compiler_params=pltpu.CompilerParams(collective_id=0, has_side_effects=True, vmem_limit_bytes=32 << 20),
        name="main",
    )(*[pltpu.with_memory_space_constraint(a, pltpu.HBM) for a in (descriptors, coefficients, whitening, targets)])
    updated = pl.pallas_call(
        store_kernel,
        out_shape=jax.ShapeDtypeStruct((ROWS, COLS), F32),
        in_specs=[vm],
        out_specs=hbm,
        scratch_shapes=[dma((8,))],
        compiler_params=pltpu.CompilerParams(vmem_limit_bytes=16 << 20),
        name="store",
    )(kern)
    return updated, residual


def solution(mesh):
    in_specs = (P(("row", "col"), None), P("col", None), P(("row", "col"), None), P())
    out_specs = (P("row", "col"), P(("row", "col"), None))
    return jax.shard_map(body, mesh=mesh, in_specs=in_specs, out_specs=out_specs, check_vma=False)
```
